256 devices in a mesh: rows: 32 (over z, x), tensor: 8 (over y, core).
Axes of the slice: x: 4, y: 4, z: 8, core: 2. Of those that a mesh axis runs over, the one named last changes fastest.
Arguments:
- context: bfloat16 [2, 5120, 4096], P(None, 'rows', 'tensor'), may hold values from -6 to 6
- o_weight: bfloat16 [4096, 8192], P('tensor'), may hold values from -0.125 to 0.125
- residual: bfloat16 [2, 5120, 8192], P(None, 'rows', 'tensor'), may hold values from -6 to 6
- counts: int32 [2, 1024], P(None, 'rows'), may hold values from 0 to 5
- slots: int32 [2, 5120], P(None, 'rows'), may hold values from 0 to 5119, as said below
- fc_weight: bfloat16 [2048, 8192], P('rows', 'tensor'), may hold values from -0.0625 to 0.0625
- gain: float32 [2048], replicated, may hold values from 0.1 to 1.9
- goal: bfloat16 [2, 5120, 2048], P(None, 'rows'), may hold values from -6 to 6
Outputs:
- verified: float32 [2, 5120, 8192], P(None, 'rows', 'tensor')
- draft_out: float32 [2, 5120, 2048], P(None, 'rows', 'tensor')
- fc_grad: float32 [2048, 8192], P('rows', 'tensor')
The draws below stay inside these ranges and needn't reach their ends.
Inputs may be any that keep to these rules, and one draw needn't show every extreme that they name: In each step the slots of all rows are a permutation of 0 to 5119. Slot i belongs to trainer device i // 160; the rows of device p take, on every trainer device, exactly the 5 slots from p * 5 to (p + 1) * 5 - 1 of that device's block.
All inputs are finite; a program needn't handle non-finite values.
Results may differ from the reference program's by a relative error of at most 0.014.
Values may be sent and summed in bfloat16 or wider, within the bound.
No kernel may reach another device: no remote copies, remote signals or barrier semaphores. Data moves between devices by JAX's collectives and lax.ppermute only.
A program may use at most 64 MiB of HBM per device.

```python
import math
import jax
import jax.numpy as jnp
from jax import lax

D = 8192
DRAFT = 2048
K = 5
STEPS = 2
ROWS_DEV = 160
REQS = 1024
ROWS = 5120
QWIDTH = 4096
N_TENSOR = 8


def one_order(subkey):
    return jax.random.permutation(subkey, ROWS_DEV)


def draw_slots(key, part):
    device_count = ROWS // ROWS_DEV
    per_peer = ROWS_DEV // device_count
    keys = jax.random.split(key, STEPS * device_count)
    orders = jax.vmap(one_order)(keys).astype(jnp.int32)
    orders = orders.reshape(STEPS, device_count, ROWS_DEV)
    source = jnp.arange(device_count, dtype=jnp.int32)[None, :, None]
    placed = orders // per_peer * ROWS_DEV + source * per_peer + orders % per_peer
    return placed.reshape(STEPS, ROWS).astype(jnp.int32)


def touch_ends(array, stream_key, least, high):
    shape = array.shape
    place = [jax.random.randint(jax.random.fold_in(stream_key, axis), (), 0, shape[axis]) for axis in range(len(shape))]
    array = array.at[tuple(place)].set(least)
    longest = shape.index(max(shape))
    place[longest] = (place[longest] + 1) % shape[longest]
    return array.at[tuple(place)].set(high)


def with_spikes(entries, key, source, target, shards_of, factor):
    def block_of(axis_at):
        return (jnp.arange(entries.shape[axis_at]) // (entries.shape[axis_at] // shards_of)).reshape((-1,) + (1,) * (entries.ndim - 1 - axis_at))

    near = jax.random.permutation(key, shards_of)[block_of(target)]
    other_side = (block_of(target) + shards_of // 2) % shards_of
    return jnp.where((block_of(source) == near) | (block_of(source) == other_side), factor * entries, entries)


def steps_of(own_key, dims, pieces, smallest, top_value):
    def one(position, parts):
        draws = jax.random.uniform(jax.random.fold_in(jax.random.fold_in(own_key, 6), position), (parts,), jnp.float32, smallest / len(pieces), top_value / len(pieces))
        return jnp.repeat(jnp.exp(draws), dims[position] // parts).reshape((-1,) + (1,) * (len(dims) - position - 1))

    level = one(*pieces[0])
    for cut in pieces[1:]:
        level = level * one(*cut)
    return level


def noise(rng, dims, deviation, reach, cuts=(), held_as=jnp.bfloat16):
    level = steps_of(rng, dims, cuts, -0.22, 0.18) if cuts else 1.0
    array = jax.random.normal(rng, dims, jnp.float32) * deviation * level
    return jnp.minimum(jnp.maximum(array, -reach), reach).astype(held_as)


def bell_draw_with(rng, extent, scale, limit, pieces, heavy, kind=jnp.bfloat16):
    values = scale * jax.random.normal(rng, extent, jnp.float32)
    if pieces:
        values = values * steps_of(rng, extent, pieces, -0.22, 0.18)
    return jnp.clip(with_spikes(values, jax.random.fold_in(rng, 3), *heavy), -limit, limit).astype(kind)


def setup_inputs(seed: int = 0) -> dict:
    key_list = jax.random.split(jax.random.key(seed), 9)
    return {
        "context": noise(key_list[0], (STEPS, ROWS, QWIDTH), 1.0, 6.0, ((1, 32), (2, 8))),
        "o_weight": bell_draw_with(key_list[1], (QWIDTH, D), QWIDTH ** -0.5, 0.125, ((0, 8),), (0, 1, 8, 2.0)),
        "residual": noise(key_list[2], (STEPS, ROWS, D), 1.0, 6.0, ((1, 32), (2, 8))),
        "counts": touch_ends(jax.random.randint(key_list[3], (STEPS, REQS), 0, K + 1), jax.random.fold_in(key_list[3], 1), 0, K).astype(jnp.int32),
        "slots": draw_slots(jax.random.fold_in(key_list[8], 71), 0),
        "fc_weight": noise(key_list[5], (DRAFT, D), D ** -0.5, 0.0625, ((0, 32), (1, 8))),
        "gain": jnp.clip(1.0 + 0.18 * jax.random.normal(key_list[6], (DRAFT,), jnp.float32), 0.1, 1.9),
        "goal": noise(key_list[7], (STEPS, ROWS, DRAFT), 1.0, 6.0, ((1, 32),)),
    }


epsilon = 1e-06

def draft_norm(summed, gain, goal, weight):
    mean_square = lax.optimization_barrier(jnp.mean(summed * summed, axis=-1, keepdims=True))
    inverse = lax.rsqrt(mean_square + epsilon)
    normed = summed * inverse * gain
    error = normed - goal.astype(jnp.float32)
    pulled = gain * (weight * error)
    spread = lax.optimization_barrier(jnp.mean(summed * pulled, axis=-1, keepdims=True))
    back = inverse * (pulled - summed * (inverse * inverse) * spread)
    return (normed, back.astype(jnp.bfloat16))

def reference(context, o_weight, residual, counts, slots, fc_weight, gain, goal):
    block = QWIDTH // N_TENSOR
    weight = 1.0 / math.sqrt(STEPS * ROWS)
    offsets = jnp.arange(ROWS, dtype=jnp.int32) % K
    verified = []
    drafted = []
    grad = jnp.zeros((DRAFT, D), jnp.float32)
    for step in range(STEPS):
        projected = jnp.zeros((ROWS, D), jnp.float32)
        for shard in range(N_TENSOR):
            head_terms = jnp.dot(context[step][:, shard * block:(shard + 1) * block], o_weight[shard * block:(shard + 1) * block], preferred_element_type=jnp.float32)
            rounded = lax.optimization_barrier(head_terms.astype(jnp.bfloat16))
            projected = projected + rounded.astype(jnp.float32)
        full_state = residual[step].astype(jnp.float32) + projected
        verified.append(full_state)
        hidden = full_state.astype(jnp.bfloat16)
        accepted = offsets < jnp.repeat(counts[step], K)
        masked = jnp.where(accepted[:, None], hidden, jnp.zeros_like(hidden))
        trained = jnp.zeros_like(masked).at[slots[step]].set(masked)
        summed = jnp.dot(trained, fc_weight.T, preferred_element_type=jnp.float32)
        normed, back = draft_norm(summed, gain, goal[step], weight)
        drafted.append(normed)
        grad = grad + jnp.dot(back.T, trained, preferred_element_type=jnp.float32)
    return (jnp.stack(verified), jnp.stack(drafted), grad)
```

```python
import functools
import math

import jax
import jax.numpy as jnp
from jax import lax
from jax.experimental import pallas as pl
from jax.experimental.pallas import tpu as pltpu
from jax.sharding import Mesh, PartitionSpec as P


K = 5
STEPS = 2
NZ, NX, NY, NC = 8, 4, 4, 2
EPSILON = 1e-06
BF16 = jnp.bfloat16
F32 = jnp.float32
VMEM = pl.BlockSpec(memory_space=pltpu.VMEM)
SMEM = pl.BlockSpec(memory_space=pltpu.SMEM)


def shift(value, axis, size, by):
    return lax.ppermute(value, axis, [(i, (i + by) % size) for i in range(size)])


def swap(value):
    return shift(value, "c", NC, 1)


def exchange(value, axis):
    return lax.all_to_all(value, axis, 0, 0, tiled=True)


def take(value, index, axis=0):
    return lax.dynamic_index_in_dim(value, index, axis, False)


def project_kernel(blocks, parts, adds, place_ref, ctx_ref, weight_ref, *refs):
    added, outs, (held, sems) = refs[:adds], list(refs[adds:-2]), refs[-2:]
    width = held.shape[2]
    count = len(blocks)
    copies = []
    for i, (d, other) in enumerate(blocks):
        core = 1 - place_ref[1] if other else place_ref[1]
        block = lax.rem(place_ref[0] + d, NY) * NC + core
        span = pl.ds(pl.multiple_of(block * width, width), width)
        copies.append(pltpu.make_async_copy(weight_ref.at[:, span], held.at[i], sems.at[i]))
        copies[-1].start()
    for i in range(count):
        copies[i].wait()
        product = jnp.dot(ctx_ref[...], held[i], preferred_element_type=F32)
        if adds:
            product = product + added[i][...].astype(F32)
        step = width // parts[i]
        for h in range(parts[i]):
            out = outs.pop(0)
            out[...] = product[:, h * step:(h + 1) * step].astype(out.dtype)


def project(place, blocks, ctx, weight, width, added, types):
    count, (rows, depth) = len(blocks), ctx.shape
    parts = [len(t) for t in types]
    return pl.pallas_call(
        functools.partial(project_kernel, blocks, parts, len(added)),
        in_specs=[SMEM, VMEM, pl.BlockSpec(memory_space=pl.ANY)] + [VMEM] * len(added),
        out_specs=[VMEM] * sum(parts),
        out_shape=[jax.ShapeDtypeStruct((rows, width // len(ts)), t) for ts in types for t in ts],
        scratch_shapes=[
            pltpu.VMEM((count, depth, width), weight.dtype),
            pltpu.SemaphoreType.DMA((count,)),
        ],
        cost_estimate=pl.CostEstimate(
            flops=2 * count * rows * depth * width,
            bytes_accessed=2 * count * (depth + rows) * width,
            transcendentals=0,
        ),
        name="project",
    )(place, ctx, weight, *added)


def merge_kernel(near_up, far_up, early_up, early_down, near_down, far_down, up, down):
    half = near_up.shape[1]
    up[:, :half] = (near_up[...] + far_up[...].astype(F32)).astype(up.dtype)
    up[:, half:] = early_up[...]
    down[:, :half] = early_down[...]
    down[:, half:] = (near_down[...] + far_down[...].astype(F32)).astype(down.dtype)


def merge(*parts):
    rows, half = parts[0].shape
    return pl.pallas_call(
        merge_kernel,
        in_specs=[VMEM] * len(parts),
        out_specs=[VMEM] * 2,
        out_shape=[jax.ShapeDtypeStruct((rows, 2 * half), BF16)] * 2,
        cost_estimate=pl.CostEstimate(flops=rows * half, bytes_accessed=18 * rows * half, transcendentals=0),
        name="merge",
    )(*parts)


def local(context, o_weight, residual, counts, slots, fc_weight, gain, goal):
    z, x, y, c = (lax.axis_index(name) for name in ("z", "x", "y", "c"))
    rows = context.shape[1]
    width = residual.shape[2]
    per_peer = rows // (NZ * NX)
    feats = fc_weight.shape[0]
    some = NZ * feats
    draft_width = gain.shape[0]
    weight = 1.0 / math.sqrt(STEPS * rows * NZ * NX)

    ctx = context.reshape(STEPS * rows, context.shape[2])
    half = width // 2
    place = jnp.stack([y, c]).astype(jnp.int32)
    blocks = ((2, True), (2, False), (1, True), (3, True), (0, True))
    first, *far_own, one, three, zero = project(
        place, blocks, ctx, o_weight, width, [], [[BF16], [F32, F32], [BF16], [BF16], [BF16]]
    )
    first, one, three, zero = swap(first), swap(one), swap(three), swap(zero)
    far = [(far_own[h] + first[:, h * half:(h + 1) * half].astype(F32)).astype(BF16) for h in range(2)]
    near = project(
        place, ((1, False), (3, False)), ctx, o_weight, width, [one, three], [[F32, BF16], [BF16, F32]]
    )
    own = project(place, ((0, False),), ctx, o_weight, width, [zero], [[F32]])[0]

    far_up = shift(far[0], "y", NY, 1)
    far_down = shift(far[1], "y", NY, -1)
    up, down = merge(near[0], far_up, near[1], near[2], near[3], far_down)
    up, down, fc_weight, goal = lax.optimization_barrier((up, down, fc_weight, goal))
    up = shift(up, "y", NY, 1)
    down = shift(down, "y", NY, -1)

    slot = per_peer + -per_peer % 8
    chosen = jnp.arange(NZ * slot, dtype=jnp.int32)
    chosen = jnp.where(chosen % slot < per_peer, (chosen // slot * NX + y) * per_peer + chosen % slot, -1)
    chosen = (chosen[:, None] == jnp.arange(rows, dtype=jnp.int32)).astype(BF16)
    target = jnp.dot(chosen, take(goal, c), preferred_element_type=F32).astype(BF16)
    cuts = [target[:, i:i + width].reshape(NZ, slot, width) for i in range(0, draft_width, width)]
    load = jnp.concatenate([jnp.broadcast_to(fc_weight, (NZ, feats, width)), *cuts], 1)
    load = exchange(load, "z")
    fc_all = load[:, :feats].reshape(some, width)
    cuts = [load[:, feats + i * slot:feats + (i + 1) * slot] for i in range(draft_width // width)]
    target = jnp.concatenate(cuts, 2).reshape(NZ * slot, NZ, NX, feats).transpose(2, 0, 1, 3)
    target = exchange(target.reshape(NX, NZ * slot, some), "x").reshape(-1, some)
    packed = jnp.arange(rows, dtype=jnp.int32)
    peer = packed // per_peer
    packed = (peer % NX * NZ + peer // NX) * slot + packed % per_peer
    packed = packed[:, None] == jnp.arange(target.shape[0], dtype=jnp.int32)
    target = jnp.dot(packed.astype(BF16), target, preferred_element_type=F32)

    source = z * NX + x
    position = slots // rows * per_peer + slots % rows - source * per_peer
    accepted = jnp.arange(rows, dtype=jnp.int32) % K < jnp.repeat(counts, K, axis=1)
    position = jnp.where(accepted, position, -1)
    pick = (position[:, None, :] == jnp.arange(rows, dtype=jnp.int32)[None, :, None]).astype(BF16)

    total = own + up.astype(F32) + down.astype(F32)
    verified = residual.astype(F32) + total.reshape(STEPS, rows, width)
    own = lax.dot_general(
        pick, verified.astype(BF16), (((2,), (1,)), ((0,), (0,))), preferred_element_type=F32
    ).astype(BF16)

    right = shift(own, "x", NX, -1)
    left = shift(own, "x", NX, 1)
    opposite = jnp.concatenate([shift(right[:1], "x", NX, -1), shift(left[1:], "x", NX, 1)], 0)
    trained = jnp.stack([own, right, opposite, left])
    trained, target = lax.optimization_barrier((trained.reshape(NX * STEPS * rows, width), target))

    partial = lax.dot_general(
        trained, fc_all, (((1,), (1,)), ((), ())), preferred_element_type=F32
    ).astype(BF16).reshape(NX, STEPS, rows, some)
    given = swap(take(partial, 1 - c, 1))
    kept = take(partial, c, 1)

    def term(i):
        m = (i - x + NX) % NX
        return (take(kept, m).astype(F32) + take(given, m).astype(F32)).astype(BF16)

    summed = jnp.stack([term(i) for i in range(NY)])
    summed = exchange(summed, "y").astype(F32).sum(0)

    scale = take(gain.reshape(NZ, NX, feats), x, 1).reshape(1, some)
    scaled = summed * scale
    sums = jnp.stack(
        [jnp.sum(summed * summed, -1), jnp.sum(scaled * scaled, -1), jnp.sum(scaled * target, -1)]
    )
    sums = exchange(jnp.broadcast_to(sums, (NX, *sums.shape)), "x").sum(0)
    mean_square, gained, aimed = sums[0] / draft_width, sums[1] / draft_width, sums[2] / draft_width
    inverse = lax.rsqrt(mean_square + EPSILON)[:, None]
    spread = weight * (inverse * gained[:, None] - aimed[:, None])
    normed = summed * inverse * scale
    pulled = scale * (weight * (normed - target))
    back = (inverse * (pulled - summed * (inverse * inverse) * spread)).astype(BF16)

    normed = normed.astype(BF16)
    pair = NC * feats
    load = jnp.stack([jnp.concatenate([back, normed[:, i * pair:(i + 1) * pair]], 1) for i in range(NY)])
    load = exchange(load, "y")
    both = jnp.stack([load, swap(load)])
    both = jnp.stack([take(both, (s + c) % NC) for s in range(NC)], 1)
    lined = jnp.stack([take(both, (m + x) % NX) for m in range(NX)])
    terms = lax.dot_general(
        lined[:, :, :, :some].reshape(NX * STEPS * rows, some),
        trained,
        (((0,), (0,)), ((), ())),
        preferred_element_type=F32,
    )

    def block(m):
        return lax.dynamic_slice_in_dim(terms, (z + m) % NZ * feats, feats, 0)

    grad = block(0)
    arrived = {m: shift(block(m).astype(BF16), "z", NZ, m) for m in (4, 3, 5, 2, 6, 1)}
    arrived[7] = shift(block(7).astype(BF16), "z", NZ, 7)
    for m in (1, 7, 2, 6, 3, 5, 4):
        grad = grad + arrived[m].astype(F32)

    out = lax.dynamic_slice_in_dim(both[:, :, :, some:], c * feats, feats, 3)
    out = out.reshape(NX * STEPS, NZ * NX, per_peer, feats).transpose(1, 0, 2, 3)
    out = exchange(out.reshape(NZ * NX, NX * STEPS * per_peer, feats), ("z", "x"))
    out = out.reshape(NZ, NX, NX, STEPS, per_peer, feats).transpose(3, 0, 2, 4, 1, 5)
    draft_out = out.reshape(STEPS, rows, NX * feats).astype(F32)
    return verified, draft_out, grad


def solution(mesh):
    grid = Mesh(mesh.devices.reshape(NZ, NX, NY, NC), ("z", "x", "y", "c"))
    r, t = ("z", "x"), ("y", "c")
    placed = (
        P(None, r, t),
        P(t, None),
        P(None, r, t),
        P(None, r),
        P(None, r),
        P(r, t),
        P(),
        P(None, r, None),
    )

    return jax.shard_map(
        local,
        mesh=grid,
        in_specs=placed,
        out_specs=(P(None, r, t), P(None, r, t), P(r, t)),
        check_vma=False,
    )
```

```python
import functools
import math

import jax
import jax.numpy as jnp
from jax import lax
from jax.experimental import pallas as pl
from jax.experimental.pallas import tpu as pltpu
from jax.sharding import Mesh, PartitionSpec as P


K = 5
STEPS = 2
NZ, NX, NY, NC = 8, 4, 4, 2
EPSILON = 1e-06
BF16 = jnp.bfloat16
F32 = jnp.float32
VMEM = pl.BlockSpec(memory_space=pltpu.VMEM)
SMEM = pl.BlockSpec(memory_space=pltpu.SMEM)


def shift(value, axis, size, by):
    return lax.ppermute(value, axis, [(i, (i + by) % size) for i in range(size)])


def swap(value):
    return shift(value, "c", NC, 1)


def exchange(value, axis):
    return lax.all_to_all(value, axis, 0, 0, tiled=True)


def take(value, index, axis=0):
    return lax.dynamic_index_in_dim(value, index, axis, False)


def project_kernel(blocks, split, adds, ctx_ref, weight_ref, *refs):
    added, outs, (held, sems) = refs[:adds], list(refs[adds:-2]), refs[-2:]
    rows, width = ctx_ref.shape[0], held.shape[2]
    y, c = lax.axis_index("y"), lax.axis_index("c")
    copies = []
    for i, (d, other) in enumerate(blocks):
        block = lax.rem(y + d, NY) * NC + (1 - c if other else c)
        span = pl.ds(pl.multiple_of(block * width, width), width)
        copies.append(pltpu.make_async_copy(weight_ref.at[:, span], held.at[i], sems.at[i]))
        copies[-1].start()
    for i in range(len(blocks)):
        copies[i].wait()
        tile = width // 2

        @pl.loop(0, width // tile)
        def _(t):
            span = pl.ds(pl.multiple_of(t * tile, tile), tile)
            product = jnp.dot(ctx_ref[...], held[i, :, span], preferred_element_type=F32)
            if i < adds:
                product = product + added[i][:, span].astype(F32)
            for s in range(split):
                step = rows // split
                outs[i * split + s][:, span] = product[s * step:(s + 1) * step].astype(BF16)


def project(blocks, ctx, weight, width, added=(), split=1):
    count, (rows, depth) = len(blocks), ctx.shape
    return pl.pallas_call(
        functools.partial(project_kernel, blocks, split, len(added)),
        in_specs=[VMEM, pl.BlockSpec(memory_space=pl.ANY)] + [VMEM] * len(added),
        out_specs=[VMEM] * (count * split),
        out_shape=[jax.ShapeDtypeStruct((rows // split, width), BF16)] * (count * split),
        scratch_shapes=[
            pltpu.VMEM((count, depth, width), weight.dtype),
            pltpu.SemaphoreType.DMA((count,)),
        ],
        cost_estimate=pl.CostEstimate(
            flops=2 * count * rows * depth * width,
            bytes_accessed=2 * count * (depth + rows) * width,
            transcendentals=0,
        ),
        name="project",
    )(ctx, weight, *added)


def local(context, o_weight, residual, counts, slots, fc_weight, gain, goal):
    z, x, y, c = (lax.axis_index(name) for name in ("z", "x", "y", "c"))
    rows = context.shape[1]
    width = residual.shape[2]
    per_peer = rows // (NZ * NX)
    feats = fc_weight.shape[0]
    some = NZ * feats
    draft_width = gain.shape[0]
    weight = 1.0 / math.sqrt(STEPS * rows * NZ * NX)

    ctx = context.reshape(STEPS * rows, context.shape[2])
    first, far_own, one, three = project(
        ((2, True), (2, False), (1, True), (3, True)), ctx, o_weight, width
    )
    first, one, three = swap(first), swap(one), swap(three)
    far = (far_own.astype(F32) + first.astype(F32)).astype(BF16).reshape(STEPS, rows, width)
    *near, zero_0, zero_1, own_0, own_1 = project(
        ((1, False), (3, False), (0, True), (0, False)), ctx, o_weight, width, (one, three), STEPS
    )
    own, zero = (own_0, own_1), [swap(v) for v in (zero_0, zero_1)]

    totals = []
    for s in range(STEPS):
        total = shift(far[s], "y", NY, 2).astype(F32)
        total = total + shift(near[s], "y", NY, 1).astype(F32)
        total = total + shift(near[STEPS + s], "y", NY, -1).astype(F32)
        totals.append(total + own[s].astype(F32) + zero[s].astype(F32))
    states = [residual[s].astype(F32) + totals[s] for s in range(STEPS)]
    verified = jnp.stack(states)

    slot = per_peer + -per_peer % 8
    chosen = jnp.arange(NZ * slot, dtype=jnp.int32)
    chosen = jnp.where(chosen % slot < per_peer, (chosen // slot * NX + y) * per_peer + chosen % slot, -1)
    chosen = (chosen[:, None] == jnp.arange(rows, dtype=jnp.int32)).astype(BF16)
    target = jnp.dot(chosen, take(goal, c), preferred_element_type=F32).astype(BF16)
    cuts = [target[:, i:i + width].reshape(NZ, slot, width) for i in range(0, draft_width, width)]
    load = jnp.concatenate([jnp.broadcast_to(fc_weight, (NZ, feats, width)), *cuts], 1)
    load = exchange(load, "z")
    fc_all = load[:, :feats].reshape(some, width)
    cuts = [load[:, feats + i * slot:feats + (i + 1) * slot] for i in range(draft_width // width)]
    target = jnp.concatenate(cuts, 2).reshape(NZ * slot, NZ, NX, feats).transpose(2, 0, 1, 3)
    target = target.reshape(NX, NZ * slot, some)
    pieces = [take(target, x)]
    for m in range(1, NX):
        piece = take(target, (x + m) % NX)
        pieces.append(shift(piece, "x", NX, m))
    target = jnp.concatenate(pieces, 0)
    packed = jnp.arange(rows, dtype=jnp.int32)
    peer = packed // per_peer
    packed = ((x + NX - peer % NX) % NX * NZ + peer // NX) * slot + packed % per_peer
    packed = packed[:, None] == jnp.arange(target.shape[0], dtype=jnp.int32)
    target = jnp.dot(packed.astype(BF16), target, preferred_element_type=F32)

    source = z * NX + x
    position = slots // rows * per_peer + slots % rows - source * per_peer
    accepted = jnp.arange(rows, dtype=jnp.int32) % K < jnp.repeat(counts, K, axis=1)
    position = jnp.where(accepted, position, -1)
    pick = (position[:, None, :] == jnp.arange(rows, dtype=jnp.int32)[None, :, None]).astype(BF16)

    trained, partial = [], []
    for s in range(STEPS):
        mine = jnp.dot(pick[s], states[s].astype(BF16), preferred_element_type=F32).astype(BF16)
        mine = lax.optimization_barrier(mine)
        around = [mine] + [shift(mine, "x", NX, -m) for m in range(1, NX)]
        trained.append(jnp.concatenate(around, 0))
        product = lax.dot_general(
            trained[s], fc_all, (((1,), (1,)), ((), ())), preferred_element_type=F32
        ).astype(BF16)
        partial.append(lax.optimization_barrier(product) if s == 0 else product)

    given = swap(jnp.where(c == 0, partial[1], partial[0])).reshape(NX, rows, some)
    kept = jnp.where(c == 0, partial[0], partial[1]).reshape(NX, rows, some)

    def term(i):
        m = (i - x + NX) % NX
        return (take(kept, m).astype(F32) + take(given, m).astype(F32)).astype(BF16)

    summed = jnp.stack([term(i) for i in range(NY)])
    summed = exchange(summed, "y").astype(F32).sum(0)

    scale = take(gain.reshape(NZ, NX, feats), x, 1).reshape(1, some)
    scaled = summed * scale
    sums = jnp.stack(
        [jnp.sum(summed * summed, -1), jnp.sum(scaled * scaled, -1), jnp.sum(scaled * target, -1)]
    )
    sums = sums + shift(sums, "x", NX, 2) + shift(sums, "x", NX, 1) + shift(sums, "x", NX, 3)
    mean_square, gained, aimed = sums[0] / draft_width, sums[1] / draft_width, sums[2] / draft_width
    inverse = lax.rsqrt(mean_square + EPSILON)[:, None]
    spread = weight * (inverse * gained[:, None] - aimed[:, None])
    normed = summed * inverse * scale
    pulled = scale * (weight * (normed - target))
    back = (inverse * (pulled - summed * (inverse * inverse) * spread)).astype(BF16)

    normed = normed.astype(BF16)
    pair = NC * feats
    load = jnp.stack([jnp.concatenate([back, normed[:, i * pair:(i + 1) * pair]], 1) for i in range(NY)])
    load = exchange(load, "y")
    both = jnp.stack([load, swap(load)])
    both = jnp.stack([take(both, (s + c) % NC) for s in range(NC)])
    lined = jnp.stack([take(both, (m + x) % NX, 1) for m in range(NX)], 1)

    def term(s):
        return lax.dot_general(
            lined[s, :, :, :some].reshape(NX * rows, some),
            trained[s],
            (((0,), (0,)), ((), ())),
            preferred_element_type=F32,
        )

    terms = term(0) + term(1)

    def block(m):
        return lax.dynamic_slice_in_dim(terms, (z + m) % NZ * feats, feats, 0)

    grad = block(0)
    arrived = {}
    for m in (4, 3, 5, 2, 6, 1):
        arrived[m] = shift(block(m).astype(BF16), "z", NZ, m)
    for m in (7,):
        arrived[m] = shift(block(m).astype(BF16), "z", NZ, m)
    for m in (1, 7, 2, 6, 3, 5, 4):
        grad = grad + arrived[m].astype(F32)

    out = lax.dynamic_slice_in_dim(both[:, :, :, some:], c * feats, feats, 3)
    out = out.reshape(STEPS * NX, NZ * NX, per_peer, feats).transpose(1, 0, 2, 3)
    out = exchange(out.reshape(NZ * NX, NX * STEPS * per_peer, feats), ("z", "x"))
    out = out.reshape(NZ, NX, STEPS, NX, per_peer, feats).transpose(2, 0, 3, 4, 1, 5)
    draft_out = out.reshape(STEPS, rows, NX * feats).astype(F32)
    return verified, draft_out, grad


def solution(mesh):
    grid = Mesh(mesh.devices.reshape(NZ, NX, NY, NC), ("z", "x", "y", "c"))
    r, t = ("z", "x"), ("y", "c")
    placed = (
        P(None, r, t),
        P(t, None),
        P(None, r, t),
        P(None, r),
        P(None, r),
        P(r, t),
        P(),
        P(None, r, None),
    )

    return jax.shard_map(
        local,
        mesh=grid,
        in_specs=placed,
        out_specs=(P(None, r, t), P(None, r, t), P(r, t)),
        check_vma=False,
    )
```

```python
import functools
import math

import jax
import jax.numpy as jnp
from jax import lax
from jax.experimental import pallas as pl
from jax.experimental.pallas import tpu as pltpu
from jax.sharding import Mesh, PartitionSpec as P


K = 5
STEPS = 2
NZ, NX, NY, NC = 8, 4, 4, 2
EPSILON = 1e-06
BF16 = jnp.bfloat16
F32 = jnp.float32
VMEM = pl.BlockSpec(memory_space=pltpu.VMEM)
SMEM = pl.BlockSpec(memory_space=pltpu.SMEM)


def shift(value, axis, size, by):
    return lax.ppermute(value, axis, [(i, (i + by) % size) for i in range(size)])


def swap(value):
    return shift(value, "c", NC, 1)


def exchange(value, axis):
    return lax.all_to_all(value, axis, 0, 0, tiled=True)


def take(value, index, axis=0):
    return lax.dynamic_index_in_dim(value, index, axis, False)


def project_kernel(blocks, split, adds, ctx_ref, weight_ref, *refs):
    added, outs, (held, sems) = refs[:adds], list(refs[adds:-2]), refs[-2:]
    rows, width = ctx_ref.shape[0], held.shape[2]
    y, c = lax.axis_index("y"), lax.axis_index("c")
    copies = []
    for i, (d, other) in enumerate(blocks):
        block = lax.rem(y + d, NY) * NC + (1 - c if other else c)
        span = pl.ds(pl.multiple_of(block * width, width), width)
        copies.append(pltpu.make_async_copy(weight_ref.at[:, span], held.at[i], sems.at[i]))
        copies[-1].start()
    for i in range(len(blocks)):
        copies[i].wait()
        product = jnp.dot(ctx_ref[...], held[i], preferred_element_type=F32)
        if i < adds:
            product = product + added[i][...].astype(F32)
        for s in range(split):
            step = rows // split
            outs[i * split + s][...] = product[s * step:(s + 1) * step].astype(BF16)


def project(blocks, ctx, weight, width, added=(), split=1):
    count, (rows, depth) = len(blocks), ctx.shape
    return pl.pallas_call(
        functools.partial(project_kernel, blocks, split, len(added)),
        in_specs=[VMEM, pl.BlockSpec(memory_space=pl.ANY)] + [VMEM] * len(added),
        out_specs=[VMEM] * (count * split),
        out_shape=[jax.ShapeDtypeStruct((rows // split, width), BF16)] * (count * split),
        scratch_shapes=[
            pltpu.VMEM((count, depth, width), weight.dtype),
            pltpu.SemaphoreType.DMA((count,)),
        ],
        cost_estimate=pl.CostEstimate(
            flops=2 * count * rows * depth * width,
            bytes_accessed=2 * count * (depth + rows) * width,
            transcendentals=0,
        ),
        name="project",
    )(ctx, weight, *added)


def local(context, o_weight, residual, counts, slots, fc_weight, gain, goal):
    z, x, y, c = (lax.axis_index(name) for name in ("z", "x", "y", "c"))
    rows = context.shape[1]
    width = residual.shape[2]
    per_peer = rows // (NZ * NX)
    feats = fc_weight.shape[0]
    some = NZ * feats
    draft_width = gain.shape[0]
    weight = 1.0 / math.sqrt(STEPS * rows * NZ * NX)

    ctx = context.reshape(STEPS * rows, context.shape[2])
    first, far_own, one, three = project(
        ((2, True), (2, False), (1, True), (3, True)), ctx, o_weight, width
    )
    first, one, three = swap(first), swap(one), swap(three)
    far = (far_own.astype(F32) + first.astype(F32)).astype(BF16).reshape(STEPS, rows, width)
    *near, zero_0, zero_1, own_0, own_1 = project(
        ((1, False), (3, False), (0, True), (0, False)), ctx, o_weight, width, (one, three), STEPS
    )
    own, zero = (own_0, own_1), [swap(v) for v in (zero_0, zero_1)]

    totals = []
    for s in range(STEPS):
        total = shift(far[s], "y", NY, 2).astype(F32)
        total = total + shift(near[s], "y", NY, 1).astype(F32)
        total = total + shift(near[STEPS + s], "y", NY, -1).astype(F32)
        totals.append(total + own[s].astype(F32) + zero[s].astype(F32))
    states = [residual[s].astype(F32) + totals[s] for s in range(STEPS)]
    verified = jnp.stack(states)

    slot = per_peer + -per_peer % 8
    chosen = jnp.arange(NZ * slot, dtype=jnp.int32)
    chosen = jnp.where(chosen % slot < per_peer, (chosen // slot * NX + y) * per_peer + chosen % slot, -1)
    chosen = (chosen[:, None] == jnp.arange(rows, dtype=jnp.int32)).astype(BF16)
    target = jnp.dot(chosen, take(goal, c), preferred_element_type=F32).astype(BF16)
    cuts = [target[:, i:i + width].reshape(NZ, slot, width) for i in range(0, draft_width, width)]
    load = jnp.concatenate([jnp.broadcast_to(fc_weight, (NZ, feats, width)), *cuts], 1)
    load = exchange(load, "z")
    fc_all = load[:, :feats].reshape(some, width)
    cuts = [load[:, feats + i * slot:feats + (i + 1) * slot] for i in range(draft_width // width)]
    target = jnp.concatenate(cuts, 2).reshape(NZ * slot, NZ, NX, feats).transpose(2, 0, 1, 3)
    target = target.reshape(NX, NZ * slot, some)
    pieces = [take(target, x)]
    for m in range(1, NX):
        piece = take(target, (x + m) % NX)
        pieces.append(shift(piece, "x", NX, m))
    target = jnp.concatenate(pieces, 0)
    packed = jnp.arange(rows, dtype=jnp.int32)
    peer = packed // per_peer
    packed = ((x + NX - peer % NX) % NX * NZ + peer // NX) * slot + packed % per_peer
    packed = packed[:, None] == jnp.arange(target.shape[0], dtype=jnp.int32)
    target = jnp.dot(packed.astype(BF16), target, preferred_element_type=F32)

    source = z * NX + x
    position = slots // rows * per_peer + slots % rows - source * per_peer
    accepted = jnp.arange(rows, dtype=jnp.int32) % K < jnp.repeat(counts, K, axis=1)
    position = jnp.where(accepted, position, -1)
    pick = (position[:, None, :] == jnp.arange(rows, dtype=jnp.int32)[None, :, None]).astype(BF16)

    trained, partial = [], []
    for s in range(STEPS):
        mine = jnp.dot(pick[s], states[s].astype(BF16), preferred_element_type=F32).astype(BF16)
        mine = lax.optimization_barrier(mine)
        across = shift(mine, "x", NX, 2)
        around = [mine, shift(mine, "x", NX, -1), across, shift(mine, "x", NX, 1)]
        trained.append(jnp.concatenate(around, 0))
        product = lax.dot_general(
            trained[s], fc_all, (((1,), (1,)), ((), ())), preferred_element_type=F32
        ).astype(BF16)
        partial.append(lax.optimization_barrier(product) if s == 0 else product)

    given = swap(jnp.where(c == 0, partial[1], partial[0])).reshape(NX, rows, some)
    kept = jnp.where(c == 0, partial[0], partial[1]).reshape(NX, rows, some)

    def term(i):
        m = (i - x + NX) % NX
        return (take(kept, m).astype(F32) + take(given, m).astype(F32)).astype(BF16)

    summed = jnp.stack([term(i) for i in range(NY)])
    summed = exchange(summed, "y").astype(F32).sum(0)

    scale = take(gain.reshape(NZ, NX, feats), x, 1).reshape(1, some)
    scaled = summed * scale
    sums = jnp.stack(
        [jnp.sum(summed * summed, -1), jnp.sum(scaled * scaled, -1), jnp.sum(scaled * target, -1)]
    )
    sums = sums + shift(sums, "x", NX, 2) + shift(sums, "x", NX, 1) + shift(sums, "x", NX, 3)
    mean_square, gained, aimed = sums[0] / draft_width, sums[1] / draft_width, sums[2] / draft_width
    inverse = lax.rsqrt(mean_square + EPSILON)[:, None]
    spread = weight * (inverse * gained[:, None] - aimed[:, None])
    normed = summed * inverse * scale
    pulled = scale * (weight * (normed - target))
    back = (inverse * (pulled - summed * (inverse * inverse) * spread)).astype(BF16)

    normed = normed.astype(BF16)
    pair = NC * feats
    load = jnp.stack([jnp.concatenate([back, normed[:, i * pair:(i + 1) * pair]], 1) for i in range(NY)])
    load = exchange(load, "y")
    both = jnp.stack([load, swap(load)])
    both = jnp.stack([take(both, (s + c) % NC) for s in range(NC)])
    lined = jnp.stack([take(both, (m + x) % NX, 1) for m in range(NX)], 1)

    def term(s):
        return lax.dot_general(
            lined[s, :, :, :some].reshape(NX * rows, some),
            trained[s],
            (((0,), (0,)), ((), ())),
            preferred_element_type=F32,
        )

    terms = term(0) + term(1)

    def block(m):
        return lax.dynamic_slice_in_dim(terms, (z + m) % NZ * feats, feats, 0)

    grad = block(0)
    arrived = {}
    for m in (4, 3, 5, 2, 6, 1):
        arrived[m] = shift(block(m).astype(BF16), "z", NZ, m)
    for m in (7,):
        arrived[m] = shift(block(m).astype(BF16), "z", NZ, m)
    for m in (1, 7, 2, 6, 3, 5, 4):
        grad = grad + arrived[m].astype(F32)

    out = lax.dynamic_slice_in_dim(both[:, :, :, some:], c * feats, feats, 3)
    out = out.reshape(STEPS * NX, NZ * NX, per_peer, feats).transpose(1, 0, 2, 3)
    out = exchange(out.reshape(NZ * NX, NX * STEPS * per_peer, feats), ("z", "x"))
    out = out.reshape(NZ, NX, STEPS, NX, per_peer, feats).transpose(2, 0, 3, 4, 1, 5)
    draft_out = out.reshape(STEPS, rows, NX * feats).astype(F32)
    return verified, draft_out, grad


def solution(mesh):
    grid = Mesh(mesh.devices.reshape(NZ, NX, NY, NC), ("z", "x", "y", "c"))
    r, t = ("z", "x"), ("y", "c")
    placed = (
        P(None, r, t),
        P(t, None),
        P(None, r, t),
        P(None, r),
        P(None, r),
        P(r, t),
        P(),
        P(None, r, None),
    )

    return jax.shard_map(
        local,
        mesh=grid,
        in_specs=placed,
        out_specs=(P(None, r, t), P(None, r, t), P(r, t)),
        check_vma=False,
    )
```
